1024 devices in a mesh: dp: 16 (over y_lo, x, core), expert: 64 (over y_hi, z).
Axes of the slice: x: 4, y: 4 (y_hi: 2, y_lo: 2; y = y_hi * 2 + y_lo), z: 32, core: 2. Of those that a mesh axis runs over, the one named last changes fastest.
Arguments:
- grad_out: bfloat16 [8192, 4096], P('expert', 'dp'), may hold values from -6 to 6
- routing: int32 [8192, 6], P('expert'), may hold values from 0 to 63, all different within a row; in each aligned block of 128 rows (0 to 127, 128 to 255, ...) at most 14 rows name the same one
- gates: float32 [8192, 6], P('expert'), may hold values from 0.05 to 1
- scales: float32 [8192], P('expert'), may hold values from 0.25 to 4
- saved_gate: bfloat16 [64, 1408, 896], P('expert'), may hold values from -6 to 6
- saved_up: bfloat16 [64, 1408, 896], P('expert'), may hold values from -6 to 6
- w_gate: bfloat16 [64, 4096, 1408], P('expert', 'dp'), may hold values from -0.09375 to 0.09375
- w_up: bfloat16 [64, 4096, 1408], P('expert', 'dp'), may hold values from -0.09375 to 0.09375
- w_down: bfloat16 [64, 1408, 4096], P('expert', None, 'dp'), may hold values from -0.15625 to 0.15625
Outputs:
- grad_x: bfloat16 [8192, 4096], P('expert', 'dp')
- grad_down: bfloat16 [64, 1408, 4096], P('expert', None, 'dp')
The draws below stay inside these ranges and needn't reach their ends.
Inputs may be any that keep to these rules, and one draw needn't show every extreme that they name: `routing`: each row names 6 different experts; within each token group of 128 rows no expert is named more than 14 times, a bound that some block reaches.
All inputs are finite; a program needn't handle non-finite values.
Results may differ from the reference program's by a relative error of at most 0.027.
Values may be sent and summed in bfloat16 or wider, within the bound.
A program may use at most 32 MiB of HBM per device.

```python
import math
import jax
import jax.numpy as jnp
import numpy as np
from jax import lax

D = 4096
FF = 1408
TOPK = 6
TOK_DEV = 128
EXPERTS = 64
CAP = 14
SLOTS = 896
TOKENS = 8192
N_DP = 16
N_EXPERT = 64


def steps_of(own_key, extent, shards, low, top_value):
    gain, own = 1.0, jax.random.fold_in(own_key, 6)
    for dim, blocks in shards:
        steps = jnp.exp(jax.random.uniform(jax.random.fold_in(own, dim), (blocks,), jnp.float32, low / len(shards), top_value / len(shards)))
        gain = gain * jnp.repeat(steps, extent[dim] // blocks).reshape([-1 if axis == dim else 1 for axis in range(len(extent))])
    return gain


def deal_out(key, own, number, rows, number_of, top, bound, slope):
    order = jax.random.permutation(key, number_of)
    crowded, usual = portions_of(number_of, rows * top, bound, slope, True), portions_of(number_of, rows * top, bound, slope, False)
    places = jnp.arange(number_of)

    def named(tallies, turn):
        used = int((tallies > 0).sum())
        fixed = max(1, used // 4)
        passed = fixed + (places - fixed + turn * (used - fixed)) % max(1, number_of - fixed)
        return jnp.zeros((number_of,), jnp.int32).at[order[jnp.where(places < fixed, places, passed)]].set(jnp.asarray(tallies, jnp.int32))

    tallies = jnp.where(number % 4 == 0, named(crowded, number // 4), named(usual, number - number // 4 - 1))
    mixed = jax.random.permutation(jax.random.fold_in(own, 3), number_of)
    source_of, sink = mixed[0:number_of // 2 * 2:2], mixed[1:number_of // 2 * 2:2]
    room = jnp.minimum(tallies[source_of] - 1, bound - tallies[sink]) // 2
    room = jnp.where((source_of == order[0]) | (sink == order[0]) | (tallies[sink] == 0), 0, jnp.maximum(room, 0))
    passed = jax.random.randint(jax.random.fold_in(own, 4), (number_of // 2,), 0, 1 << 20) % (room + 1)
    tallies = tallies.at[source_of].add(-passed).at[sink].add(passed)
    labels = jnp.searchsorted(jnp.cumsum(tallies), jnp.arange(rows * top), side="right").astype(jnp.int32)
    grid = labels.reshape(top, rows).T
    grid = grid[jax.random.permutation(jax.random.fold_in(own, 1), rows)]
    turn = jax.random.randint(jax.random.fold_in(own, 2), (rows, 1), 0, top)
    return jnp.take_along_axis(grid, (jnp.arange(top)[None, :] + turn) % top, axis=1)


def portions_of(number_of, total, limit, lean, full):
    portions = [(1 << 20) // math.isqrt(standing ** lean) + 1 for standing in range(1, number_of + 1)]
    largest = limit if full else min(limit, max(-(-total // number_of), total * portions[0] // sum(portions)))
    least = 1 if total - largest >= number_of - 1 else 0
    counts, surplus = [largest] + [least] * (number_of - 1), total - largest - least * (number_of - 1)
    while surplus > 0:
        movable = [i for i in range(1, number_of) if counts[i] < largest] or [i for i in range(1, number_of) if counts[i] < limit]
        mass, remaining = sum([portions[i] for i in movable]), surplus
        for i in movable:
            addition = min(limit - counts[i], max(1, remaining * portions[i] // mass), surplus)
            counts[i] = counts[i] + addition
            surplus = surplus - addition
    return np.array(counts)


def gaussian(stream_key, dims, deviation, bound, shards=(), kind=jnp.bfloat16):
    values = jax.random.normal(stream_key, dims, jnp.float32) * deviation
    if len(shards) > 0:
        values = steps_of(stream_key, dims, shards, -0.22, 0.18) * values
    return jnp.clip(values, min=-bound, max=bound).astype(kind)


def setup_inputs(seed: int = 0) -> dict:
    streams_of = jax.random.split(jax.random.key(seed), 10)
    grad_out = gaussian(streams_of[0], (TOKENS, D), 1.0, 6.0, ((0, 64), (1, 16)))
    routing_keys = jax.random.split(jax.random.fold_in(streams_of[1], 1), TOKENS // TOK_DEV)
    routing_turns = jax.random.permutation(jax.random.fold_in(streams_of[1], 3), TOKENS // TOK_DEV)
    routing = jax.vmap(lambda own, number: deal_out(jax.random.fold_in(streams_of[1], 2), own, number, TOK_DEV, EXPERTS, TOPK, CAP, 1))(routing_keys, routing_turns).reshape((TOKENS, TOPK))
    gates = jnp.clip(jnp.exp(math.log(1.0) - 2.9957323 * jax.random.uniform(streams_of[2], (TOKENS, TOPK), jnp.float32) ** steps_of(streams_of[2], (TOKENS, TOPK), ((0, 64),), -0.2, 0.2)), 0.05, 1.0)
    scales = jnp.clip(jnp.exp(math.log(4.0) - 2.7725887 * jax.random.uniform(streams_of[3], (TOKENS,), jnp.float32) ** steps_of(streams_of[3], (TOKENS,), ((0, 64),), -0.2, 0.2)), 0.25, 4.0)
    saved_gate = gaussian(streams_of[4], (EXPERTS, FF, SLOTS), 1.5, 6.0, ((0, 64),))
    saved_up = gaussian(streams_of[5], (EXPERTS, FF, SLOTS), 1.0, 6.0, ((0, 64),))
    w_gate = gaussian(streams_of[6], (EXPERTS, D, FF), D ** -0.5, 0.09375, ((0, 64), (1, 16)))
    w_up = gaussian(streams_of[7], (EXPERTS, D, FF), D ** -0.5, 0.09375, ((0, 64), (1, 16)))
    w_down = gaussian(streams_of[8], (EXPERTS, FF, D), FF ** -0.5, 0.15625, ((0, 64), (2, 16)))
    return dict(grad_out=grad_out, routing=routing, gates=gates, scales=scales, saved_gate=saved_gate, saved_up=saved_up, w_gate=w_gate, w_up=w_up, w_down=w_down)


def slot_positions(routing):
    rows = routing.reshape(N_EXPERT, TOK_DEV * TOPK)

    def one_group(route_row):
        hot = (route_row[:, None] == jnp.arange(EXPERTS, dtype=jnp.int32)[None, :]).astype(jnp.int32)
        return jnp.sum(hot * (jnp.cumsum(hot, axis=0) - 1), axis=1).astype(jnp.int32)

    return lax.map(one_group, rows).reshape(TOKENS, TOPK)


def reference(grad_out, routing, gates, scales, saved_gate, saved_up, w_gate, w_up, w_down):
    position = slot_positions(routing)
    group = (jnp.arange(TOKENS, dtype=jnp.int32) // TOK_DEV)[:, None]
    slot = (group * CAP + position).astype(jnp.int32)
    flat = (routing * SLOTS + slot).astype(jnp.int32)
    token_ids = jnp.broadcast_to(jnp.arange(TOKENS, dtype=jnp.int32)[:, None], (TOKENS, TOPK))
    owner = jnp.zeros((EXPERTS * SLOTS,), jnp.int32).at[flat.reshape(-1)].set(token_ids.reshape(-1))
    factor = gates * scales[:, None]
    weight = jnp.zeros((EXPERTS * SLOTS,), jnp.float32).at[flat.reshape(-1)].set(factor.reshape(-1).astype(jnp.float32))
    owner = owner.reshape(EXPERTS, SLOTS)
    weight = weight.reshape(EXPERTS, SLOTS)
    dcols = D // N_DP

    def one_expert(items):
        own, fac, sgate, sup, wgate, wup, wdown = items
        expert_grad = (fac[:, None] * grad_out[own].astype(jnp.float32)).astype(jnp.bfloat16)
        parts = jnp.einsum("sid,fid->isf", expert_grad.reshape(SLOTS, N_DP, dcols).astype(jnp.float32),
                           wdown.reshape(FF, N_DP, dcols).astype(jnp.float32))
        rounded = lax.optimization_barrier(parts.astype(jnp.bfloat16))
        hidden_grad = jnp.sum(rounded.astype(jnp.float32), axis=0).astype(jnp.bfloat16)
        g = sgate.T.astype(jnp.float32)
        u = sup.T.astype(jnp.float32)
        sig = jax.nn.sigmoid(g)
        dh = hidden_grad.astype(jnp.float32)
        gate_grad = (dh * u * sig * (1.0 + g * (1.0 - sig))).astype(jnp.bfloat16)
        up_grad = (dh * g * sig).astype(jnp.bfloat16)
        slot_grad = (jnp.dot(gate_grad.astype(jnp.float32), wgate.T.astype(jnp.float32), preferred_element_type=jnp.float32)
                     + jnp.dot(up_grad.astype(jnp.float32), wup.T.astype(jnp.float32), preferred_element_type=jnp.float32)).astype(jnp.bfloat16)
        hidden = (g * sig * u).astype(jnp.bfloat16)
        grad_down = jnp.dot(hidden.T.astype(jnp.float32), expert_grad.astype(jnp.float32),
                            preferred_element_type=jnp.float32).astype(jnp.bfloat16)
        return slot_grad, grad_down

    slot_grads, grad_down = lax.map(one_expert, (owner, weight, saved_gate, saved_up, w_gate, w_up, w_down))
    picked = slot_grads.reshape(EXPERTS * SLOTS, D)[flat]
    grad_x = jnp.sum(picked.astype(jnp.float32), axis=1).astype(jnp.bfloat16)
    return grad_x, grad_down
```

```python
import functools

import jax
import jax.numpy as jnp
from jax import lax
from jax.experimental import pallas as pl
from jax.experimental.pallas import tpu as pltpu
from jax.sharding import PartitionSpec as P

MESH = pl.DeviceIdType.MESH
PAD = 16
F32 = jnp.float32
BF16 = jnp.bfloat16


def nt(a, b):
    return lax.dot_general(a, b, (((1,), (1,)), ((), ())), preferred_element_type=F32)


def nn(a, b):
    return lax.dot_general(a, b, (((1,), (0,)), ((), ())), preferred_element_type=F32)


def iota(shape, dim):
    return lax.broadcasted_iota(jnp.int32, shape, dim)


def onehot(cond):
    return jnp.where(cond, 1.0, 0.0).astype(BF16)


def kernel(
    nz,
    cap,
    go_ref,
    rt_ref,
    gt_ref,
    sc_ref,
    sg_hbm,
    su_hbm,
    wg_hbm,
    wu_hbm,
    wd_hbm,
    gx_ref,
    gd_hbm,
    send,
    arr,
    sib,
    back,
    part,
    rsin,
    hid,
    fac_g,
    fac_u,
    sgv,
    suv,
    hact,
    wg,
    wu,
    wd,
    ret,
    gdv,
    coll_t,
    a_send,
    a_recv,
    b_send,
    b_recv,
    r_send,
    r_recv,
    g_send,
    g_recv,
    w_send,
    w_recv,
    s_send,
    s_recv,
    l_sem,
):
    tok, dcols = go_ref.shape
    topk = rt_ref.shape[1]
    ff, slots = sgv.shape
    ne = 2 * nz
    nq = part.shape[1]
    rows = part.shape[2]
    half = nq * rows
    dp = lax.axis_index("dp")
    e = lax.axis_index("expert")
    c = lax.rem(dp, 2)
    base = dp - c
    q = lax.div(dp, 2)
    yh = lax.div(e, nz)
    z = lax.rem(e, nz)
    h = lax.rem(z, 2)
    zz = lax.div(z, 2)

    barrier = pltpu.get_barrier_semaphore()

    def greet(i, carry):
        idx = lax.rem(e * 2 + c + i, 2 * ne)
        pl.semaphore_signal(
            barrier,
            inc=1,
            device_id=(base + lax.rem(idx, 2), lax.div(idx, 2)),
            device_id_type=MESH,
        )
        return carry

    lax.fori_loop(1, 2 * ne, greet, 0)
    for i in range(1, nq):
        pl.semaphore_signal(
            barrier,
            inc=1,
            device_id=(lax.rem(q + i, nq) * 2 + c, e),
            device_id_type=MESH,
        )

    loads = [
        pltpu.make_async_copy(sg_hbm.at[0], sgv, l_sem.at[0]),
        pltpu.make_async_copy(su_hbm.at[0], suv, l_sem.at[1]),
        pltpu.make_async_copy(wd_hbm.at[0], wd.at[c], l_sem.at[2]),
        pltpu.make_async_copy(wg_hbm.at[0], wg.at[c], l_sem.at[3]),
        pltpu.make_async_copy(wu_hbm.at[0], wu.at[c], l_sem.at[4]),
    ]
    for copy in loads:
        copy.start()

    lane_e = iota((tok, ne), 1)
    named = jnp.zeros((tok, ne), F32)
    gate = jnp.zeros((tok, ne), F32)
    for k in range(topk):
        hit = rt_ref[:, k : k + 1] == lane_e
        named = named + jnp.where(hit, 1.0, 0.0)
        gate = gate + jnp.where(hit, gt_ref[:, k : k + 1], 0.0)
    earlier = onehot(iota((tok, tok), 0) > iota((tok, tok), 1))
    position = nn(earlier, named.astype(BF16))
    value = (named * (position + 1.0)).astype(BF16)
    spread = (iota((ne * PAD, ne), 0) // PAD) == iota((ne * PAD, ne), 1)
    wanted = ((iota((ne * PAD, tok), 0) % PAD) + 1).astype(F32)
    pick = nt(onehot(spread), value) == wanted
    gates_at = lax.dot_general(
        jnp.where(spread, 1.0, 0.0),
        gate,
        (((1,), (1,)), ((), ())),
        precision=lax.Precision.HIGHEST,
        preferred_element_type=F32,
    )
    slot_factor = jnp.sum(
        jnp.where(pick, gates_at * sc_ref[...], 0.0), axis=1, keepdims=True
    )
    owned = nn(onehot(pick), go_ref[...])
    send[...] = (slot_factor * owned).astype(BF16)
    spread_t = iota((ne, ne * PAD), 0) == (iota((ne, ne * PAD), 1) // PAD)
    wanted_t = ((iota((tok, ne * PAD), 1) % PAD) + 1).astype(F32)
    coll_t[...] = onehot(nn(value, onehot(spread_t)) == wanted_t)

    pl.semaphore_wait(barrier, 2 * ne - 1 + nq - 1)

    other = base + 1 - c
    weights = []
    for k in range(2):
        yt = yh + k - 2 * yh * k

        def scatter(i, carry, k=k, yt=yt):
            j = nz - 1 - i
            step = lax.div(j + 1, 2) * (2 * lax.rem(j, 2) - 1)
            to = yt * nz + lax.rem(z + step + nz, nz)
            source = send.at[pl.ds(pl.multiple_of(to * PAD, PAD), PAD)]
            target = arr.at[k, c, pl.ds(pl.multiple_of(zz * PAD, PAD), PAD)]
            remote = pltpu.make_async_remote_copy(
                src_ref=source,
                dst_ref=target,
                send_sem=a_send.at[k],
                recv_sem=a_recv.at[k],
                device_id=(base + h, to),
                device_id_type=MESH,
            )
            if k == 0:
                mine = jnp.logical_and(to == e, h == c)

                @pl.when(mine)
                def _():
                    pltpu.make_async_copy(source, target, a_recv.at[k]).start()

                @pl.when(jnp.logical_not(mine))
                def _():
                    remote.start()
            else:
                remote.start()
            return carry

        lax.fori_loop(0, nz, scatter, 0)
        if k == 0:
            for n, (src, dst) in enumerate(((wd_hbm, wd), (wg_hbm, wg), (wu_hbm, wu))):
                copy = pltpu.make_async_remote_copy(
                    src_ref=src.at[0],
                    dst_ref=dst.at[c],
                    send_sem=w_send.at[n],
                    recv_sem=w_recv.at[n],
                    device_id=(other, e),
                    device_id_type=MESH,
                )
                copy.start()
                weights.append(copy)

    loads[0].wait()
    loads[1].wait()

    def slot_of(index, core):
        k = index // half
        g = (yh + k - 2 * yh * k) * nz + ((index % half) // PAD) * 2 + core
        place = index % PAD
        return jnp.where(place < cap, g * cap + place, -1)

    take = onehot(slot_of(iota((2 * half, slots), 0), c) == iota((2 * half, slots), 1))
    tile = 128

    def factors(i, carry):
        f0 = pl.multiple_of(i * tile, tile)
        g = nt(take, sgv[pl.ds(f0, tile), :])
        u = nt(take, suv[pl.ds(f0, tile), :])
        sig = jax.nn.sigmoid(g)
        fac_g[:, pl.ds(f0, tile)] = u * sig * (1.0 + g * (1.0 - sig))
        fac_u[:, pl.ds(f0, tile)] = g * sig
        return carry

    lax.fori_loop(0, ff // tile, factors, 0)

    def activate(i, carry):
        f0 = pl.multiple_of(i * 32, 32)
        g = sgv[pl.ds(f0, 32), :].astype(F32)
        u = suv[pl.ds(f0, 32), :].astype(F32)
        hact[pl.ds(f0, 32), :] = (g * jax.nn.sigmoid(g) * u).astype(BF16)
        return carry

    lax.fori_loop(0, ff // 32, activate, 0)

    for copy in loads[2:]:
        copy.wait()

    sibs = []
    for k in range(2):
        pltpu.make_async_copy(arr.at[k], arr.at[k], a_recv.at[k]).wait()
        if k == 0:
            weights[0].wait_recv()
        copy = pltpu.make_async_remote_copy(
            src_ref=arr.at[k, 1 - c],
            dst_ref=sib.at[pl.ds(k * half, half)],
            send_sem=s_send.at[k],
            recv_sem=s_recv.at[k],
            device_id=(other, e),
            device_id_type=MESH,
        )
        copy.start()
        sibs.append(copy)

        def partial_sums(i, carry, k=k):
            f0 = pl.multiple_of(i * tile, tile)
            value = nt(arr[k, 0], wd[0, pl.ds(f0, tile), :]) + nt(
                arr[k, 1], wd[1, pl.ds(f0, tile), :]
            )
            part[k, :, :, pl.ds(f0, tile)] = value.astype(BF16).reshape(nq, rows, tile)
            return carry

        lax.fori_loop(0, ff // tile, partial_sums, 0)

        def exchange(i, carry, k=k):
            to = lax.rem(q + i, nq)
            pltpu.make_async_remote_copy(
                src_ref=part.at[k, to],
                dst_ref=rsin.at[k, q],
                send_sem=r_send.at[k],
                recv_sem=r_recv.at[k],
                device_id=(to * 2 + c, e),
                device_id_type=MESH,
            ).start()
            return carry

        lax.fori_loop(1, nq, exchange, 0)
        rsin[k, q] = part[k, q]
        everyone = pl.ds(0, nq - 1)
        pltpu.make_async_copy(
            rsin.at[k, everyone], rsin.at[k, everyone], r_recv.at[k]
        ).wait()
        total = rsin[k, 0].astype(F32)
        for i in range(1, nq):
            total = total + rsin[k, i].astype(F32)
        hid[k, q] = total.astype(BF16)

        def share(i, carry, k=k):
            to = lax.rem(q + i, nq)
            pltpu.make_async_remote_copy(
                src_ref=hid.at[k, q],
                dst_ref=hid.at[k, q],
                send_sem=g_send.at[k],
                recv_sem=g_recv.at[k],
                device_id=(to * 2 + c, e),
                device_id_type=MESH,
            ).start()
            return carry

        lax.fori_loop(1, nq, share, 0)
        if k == 0:
            weights[1].wait_recv()
            weights[2].wait_recv()
        pltpu.make_async_copy(
            hid.at[k, everyone], hid.at[k, everyone], g_recv.at[k]
        ).wait()

        dh = hid[k].astype(F32).reshape(half, ff)
        gate_grad = (dh * fac_g[pl.ds(k * half, half), :]).astype(BF16)
        up_grad = (dh * fac_u[pl.ds(k * half, half), :]).astype(BF16)
        for n in range(2):
            ret[k, n] = (nt(gate_grad, wg[n]) + nt(up_grad, wu[n])).astype(BF16)

        yt = yh + k - 2 * yh * k

        def give_back(i, carry, k=k, yt=yt):
            j = nz // 2 - 1 - i
            step = lax.div(j + 1, 2) * (2 * lax.rem(j, 2) - 1)
            zt = lax.rem(zz + step + nz // 2, nz // 2)
            to = yt * nz + zt * 2 + c
            target = back.at[pl.ds(pl.multiple_of(e * PAD, PAD), PAD)]
            for n in range(2):
                source = ret.at[k, n, pl.ds(pl.multiple_of(zt * PAD, PAD), PAD)]
                remote = pltpu.make_async_remote_copy(
                    src_ref=source,
                    dst_ref=target,
                    send_sem=b_send,
                    recv_sem=b_recv,
                    device_id=(base + n, to),
                    device_id_type=MESH,
                )
                if k == 0:
                    mine = jnp.logical_and(to == e, c == n)

                    @pl.when(mine)
                    def _(source=source):
                        pltpu.make_async_copy(source, target, b_recv).start()

                    @pl.when(jnp.logical_not(mine))
                    def _(remote=remote):
                        remote.start()
                else:
                    remote.start()
            return carry

        lax.fori_loop(0, nz // 2, give_back, 0)

    sibs[0].wait_recv()
    sibs[1].wait_recv()
    own = jnp.concatenate([arr[0, c], arr[1, c]], axis=0)
    order = iota((slots, 2 * half), 1)
    slot = iota((slots, 2 * half), 0)
    natural = (
        nn(onehot(slot_of(order, c) == slot), own)
        + nn(onehot(slot_of(order, 1 - c) == slot), sib[...])
    ).astype(BF16)

    def down(i, carry):
        f0 = pl.multiple_of(i * tile, tile)
        gdv[pl.ds(f0, tile), :] = nn(hact[pl.ds(f0, tile), :], natural).astype(BF16)
        return carry

    lax.fori_loop(0, ff // tile, down, 0)
    out = pltpu.make_async_copy(gdv, gd_hbm.at[0], l_sem.at[0])
    out.start()

    pltpu.make_async_copy(back, back, b_recv).wait()
    gx_ref[...] = nn(coll_t[...], back[...]).astype(BF16)

    out.wait()
    for copy in weights + sibs:
        copy.wait_send()
    for k in range(2):
        pltpu.make_async_copy(
            rsin.at[k, pl.ds(0, nq - 1)], rsin.at[k, pl.ds(0, nq - 1)], r_send.at[k]
        ).wait()
        pltpu.make_async_copy(
            rsin.at[k, pl.ds(0, nq - 1)], rsin.at[k, pl.ds(0, nq - 1)], g_send.at[k]
        ).wait()
    less = (nz - 1) * PAD
    full = nz * PAD
    pltpu.make_async_copy(
        send.at[pl.ds(0, full)], send.at[pl.ds(0, full)], a_send.at[1]
    ).wait()

    @pl.when(h == c)
    def _():
        pltpu.make_async_copy(
            send.at[pl.ds(0, less)], send.at[pl.ds(0, less)], a_send.at[0]
        ).wait()
        pltpu.make_async_copy(
            send.at[pl.ds(0, full + less)], send.at[pl.ds(0, full + less)], b_send
        ).wait()

    @pl.when(h != c)
    def _():
        pltpu.make_async_copy(
            send.at[pl.ds(0, full)], send.at[pl.ds(0, full)], a_send.at[0]
        ).wait()
        pltpu.make_async_copy(send, send, b_send).wait()


def local(grad_out, routing, gates, scales, saved_gate, saved_up, w_gate, w_up, w_down):
    tok, dcols = grad_out.shape
    ne = lax.axis_size("expert")
    nq = lax.axis_size("dp") // 2
    nz = ne // 2
    _, ff, slots = saved_gate.shape
    cap = slots // ne
    half = nz // 2 * PAD
    rows = half // nq
    vmem = pl.BlockSpec(memory_space=pltpu.VMEM)
    hbm = pl.BlockSpec(memory_space=pl.ANY)
    dma = pltpu.SemaphoreType.DMA
    return pl.pallas_call(
        functools.partial(kernel, nz, cap),
        out_shape=(
            jax.ShapeDtypeStruct((tok, dcols), BF16),
            jax.ShapeDtypeStruct((1, ff, dcols), BF16),
        ),
        in_specs=[vmem] * 4 + [hbm] * 5,
        out_specs=(vmem, hbm),
        scratch_shapes=[
            pltpu.VMEM((ne * PAD, dcols), BF16),
            pltpu.VMEM((2, 2, half, dcols), BF16),
            pltpu.VMEM((2 * half, dcols), BF16),
            pltpu.VMEM((ne * PAD, dcols), BF16),
            pltpu.VMEM((2, nq, rows, ff), BF16),
            pltpu.VMEM((2, nq, rows, ff), BF16),
            pltpu.VMEM((2, nq, rows, ff), BF16),
            pltpu.VMEM((2 * half, ff), F32),
            pltpu.VMEM((2 * half, ff), F32),
            pltpu.VMEM((ff, slots), BF16),
            pltpu.VMEM((ff, slots), BF16),
            pltpu.VMEM((ff, slots), BF16),
            pltpu.VMEM((2, dcols, ff), BF16),
            pltpu.VMEM((2, dcols, ff), BF16),
            pltpu.VMEM((2, ff, dcols), BF16),
            pltpu.VMEM((2, 2, half, dcols), BF16),
            pltpu.VMEM((ff, dcols), BF16),
            pltpu.VMEM((tok, ne * PAD), BF16),
            dma((2,)),
            dma((2,)),
            dma,
            dma,
            dma((2,)),
            dma((2,)),
            dma((2,)),
            dma((2,)),
            dma((3,)),
            dma((3,)),
            dma((2,)),
            dma((2,)),
            dma((5,)),
        ],
        compiler_params=pltpu.CompilerParams(
            collective_id=0, has_side_effects=True, vmem_limit_bytes=56 * 1024 * 1024
        ),
    )(
        grad_out,
        routing,
        gates,
        scales.reshape(1, tok),
        saved_gate,
        saved_up,
        w_gate,
        w_up,
        w_down,
    )


def solution(mesh):
    return jax.shard_map(
        local,
        mesh=mesh,
        in_specs=(
            P("expert", "dp"),
            P("expert", None),
            P("expert", None),
            P("expert"),
            P("expert", None, None),
            P("expert", None, None),
            P("expert", "dp", None),
            P("expert", "dp", None),
            P("expert", None, "dp"),
        ),
        out_specs=(P("expert", "dp"), P("expert", None, "dp")),
        check_vma=False,
    )
```

```python
import functools

import jax
import jax.numpy as jnp
from jax import lax
from jax.experimental import pallas as pl
from jax.experimental.pallas import tpu as pltpu
from jax.sharding import PartitionSpec as P

MESH = pl.DeviceIdType.MESH
PAD = 16
PARTS = 4
F32 = jnp.float32
BF16 = jnp.bfloat16


def nt(a, b):
    return lax.dot_general(a, b, (((1,), (1,)), ((), ())), preferred_element_type=F32)


def nn(a, b):
    return lax.dot_general(a, b, (((1,), (0,)), ((), ())), preferred_element_type=F32)


def iota(shape, dim):
    return lax.broadcasted_iota(jnp.int32, shape, dim)


def onehot(cond):
    return jnp.where(cond, 1.0, 0.0).astype(BF16)


def kernel(
    nz,
    cap,
    go_ref,
    rt_ref,
    gt_ref,
    sc_ref,
    sg_hbm,
    su_hbm,
    wg_hbm,
    wu_hbm,
    wd_hbm,
    gx_ref,
    gd_hbm,
    send,
    arr,
    sib,
    back,
    part,
    rsin,
    hid,
    fac_g,
    fac_u,
    sgv,
    suv,
    hact,
    wg,
    wu,
    wd,
    ret,
    gdv,
    coll_t,
    a_send,
    a_recv,
    b_send,
    b_recv,
    r_send,
    r_recv,
    g_send,
    g_recv,
    w_send,
    w_recv,
    s_send,
    s_recv,
    l_sem,
):
    tok, dcols = go_ref.shape
    topk = rt_ref.shape[0]
    ff, slots = sgv.shape
    ne = 2 * nz
    chunks, nq, rows, _ = part.shape
    size = nq * rows
    turns = size // (2 * PAD)
    dp = lax.axis_index("dp")
    e = lax.axis_index("expert")
    c = lax.rem(dp, 2)
    base = dp - c
    q = lax.div(dp, 2)
    yh = lax.div(e, nz)
    z = lax.rem(e, nz)
    h = lax.rem(z, 2)

    def hop(t, odd):
        far = nz // 2 - odd - 2 * ((t + 1 - odd) // 2)
        return far * (2 * ((t + odd) % 2) - 1)

    barrier = pltpu.get_barrier_semaphore()

    def greet(i, carry):
        step = lax.div(i + 1, 2) * (2 * lax.rem(i, 2) - 1)
        zt = lax.rem(z + nz // 2 + step + nz, nz)
        for yt in range(2):
            there = yt * nz + zt

            @pl.when(jnp.logical_or(there != e, h != c))
            def _(there=there):
                pl.semaphore_signal(
                    barrier, inc=1, device_id=(base + h, there), device_id_type=MESH
                )

            @pl.when(
                jnp.logical_and(
                    lax.rem(zt, 2) == c, jnp.logical_or(there != e, h == c)
                )
            )
            def _(there=there):
                pl.semaphore_signal(
                    barrier, inc=1, device_id=(base + 1 - h, there), device_id_type=MESH
                )

        return carry

    lax.fori_loop(0, nz, greet, 0)
    for i in range(1, nq):
        pl.semaphore_signal(
            barrier,
            inc=1,
            device_id=(lax.rem(q + i, nq) * 2 + c, e),
            device_id_type=MESH,
        )

    loads = [
        pltpu.make_async_copy(sg_hbm.at[0], sgv, l_sem.at[0]),
        pltpu.make_async_copy(su_hbm.at[0], suv, l_sem.at[1]),
        pltpu.make_async_copy(wd_hbm.at[0], wd.at[c], l_sem.at[2]),
        pltpu.make_async_copy(wg_hbm.at[0], wg.at[c], l_sem.at[3]),
        pltpu.make_async_copy(wu_hbm.at[0], wu.at[c], l_sem.at[4]),
    ]
    for copy in loads:
        copy.start()

    row_e = iota((ne, tok), 0)
    named = jnp.zeros((ne, tok), F32)
    gate = jnp.zeros((ne, tok), F32)
    for k in range(topk):
        hit = rt_ref[k : k + 1, :] == row_e
        named = named + jnp.where(hit, 1.0, 0.0)
        gate = gate + jnp.where(hit, gt_ref[k : k + 1, :], 0.0)
    earlier = onehot(iota((tok, tok), 0) < iota((tok, tok), 1))
    value = named * (nn(named.astype(BF16), earlier) + 1.0)
    spread = (iota((ne * PAD, ne), 0) // PAD) == iota((ne * PAD, ne), 1)
    wanted = ((iota((ne * PAD, tok), 0) % PAD) + 1).astype(F32)
    pick = nn(onehot(spread), value.astype(BF16)) == wanted
    gates_at = lax.dot_general(
        jnp.where(spread, 1.0, 0.0),
        gate,
        (((1,), (0,)), ((), ())),
        precision=lax.Precision.HIGHEST,
        preferred_element_type=F32,
    )
    slot_factor = jnp.sum(
        jnp.where(pick, gates_at * sc_ref[...], 0.0), axis=1, keepdims=True
    )
    owned = nn(onehot(pick), go_ref[...])
    send[...] = (slot_factor * owned).astype(BF16)

    pl.semaphore_wait(barrier, ne + ne // 2 + nq - 1 - jnp.where(h == c, 1, 0))

    other = base + 1 - c

    def scatter(i, carry, n, last):
        k = lax.rem(i, 2)
        odd = lax.rem(lax.div(i, 2), 2)
        turn = lax.div(i, 4)
        step = hop(n * turns + turn, odd)
        to = (yh + k - 2 * yh * k) * nz + lax.rem(z - step + nz, nz)
        source = send.at[pl.ds(pl.multiple_of(to * PAD, PAD), PAD)]
        place = pl.multiple_of((turn * 2 + k) * PAD, PAD)
        target = arr.at[n, c, pl.ds(place, PAD)]
        remote = pltpu.make_async_remote_copy(
            src_ref=source,
            dst_ref=target,
            send_sem=a_send.at[n],
            recv_sem=a_recv.at[n],
            device_id=(base + h, to),
            device_id_type=MESH,
        )
        if last:
            mine = jnp.logical_and(to == e, h == c)

            @pl.when(mine)
            def _():
                pltpu.make_async_copy(source, target, a_recv.at[n]).start()

            @pl.when(jnp.logical_not(mine))
            def _():
                remote.start()
        else:
            remote.start()
        return carry

    def issue(n):
        last = n == chunks - 1
        lax.fori_loop(0, 4 * turns, functools.partial(scatter, n=n, last=last), 0)

    def left(n):
        out = pl.ds(0, 4 * turns * PAD)
        pltpu.make_async_copy(send.at[out], send.at[out], a_send.at[n]).wait()

    issue(0)
    weights = []
    for n, (src, dst) in enumerate(((wd_hbm, wd), (wg_hbm, wg), (wu_hbm, wu))):
        copy = pltpu.make_async_remote_copy(
            src_ref=src.at[0],
            dst_ref=dst.at[c],
            send_sem=w_send.at[n],
            recv_sem=w_recv.at[n],
            device_id=(other, e),
            device_id_type=MESH,
        )
        copy.start()
        weights.append(copy)

    spread_t = iota((ne, ne * PAD), 0) == (iota((ne, ne * PAD), 1) // PAD)
    wanted_t = ((iota((tok, ne * PAD), 1) % PAD) + 1).astype(F32)
    coll_t[...] = onehot(nn(value.T.astype(BF16), onehot(spread_t)) == wanted_t)

    loads[0].wait()
    loads[1].wait()

    def slot_of(index, core):
        k = (index // PAD) % 2
        odd = lax.rem(z + core, 2)
        zt = (z + hop(index // (2 * PAD), odd) + nz) % nz
        g = (yh + k - 2 * yh * k) * nz + zt
        place = index % PAD
        return jnp.where(place < cap, g * cap + place, -1)

    total = chunks * size
    take = onehot(slot_of(iota((total, 1), 0), c) == iota((total, slots), 1))
    tile = 128

    def factors(i, carry):
        f0 = pl.multiple_of(i * tile, tile)
        g = nt(take, sgv[pl.ds(f0, tile), :])
        u = nt(take, suv[pl.ds(f0, tile), :])
        sig = jax.nn.sigmoid(g)
        fac_g[:, pl.ds(f0, tile)] = u * sig * (1.0 + g * (1.0 - sig))
        fac_u[:, pl.ds(f0, tile)] = g * sig
        return carry

    lax.fori_loop(0, ff // tile, factors, 0)
    issue(1)

    def activate(i, carry):
        f0 = pl.multiple_of(i * 32, 32)
        g = sgv[pl.ds(f0, 32), :].astype(F32)
        u = suv[pl.ds(f0, 32), :].astype(F32)
        hact[pl.ds(f0, 32), :] = (g * jax.nn.sigmoid(g) * u).astype(BF16)
        return carry

    lax.fori_loop(0, ff // 32, activate, 0)

    for copy in loads[2:]:
        copy.wait()

    sibs = []
    everyone = pl.ds(0, nq - 1)

    def reduce_start(n):
        pltpu.make_async_copy(arr.at[n], arr.at[n], a_recv.at[n]).wait()
        if n == 0:
            weights[0].wait_recv()

        def partial_sums(i, carry):
            f0 = pl.multiple_of(i * tile, tile)
            value = nt(arr[n, 0], wd[0, pl.ds(f0, tile), :]) + nt(
                arr[n, 1], wd[1, pl.ds(f0, tile), :]
            )
            part[n, :, :, pl.ds(f0, tile)] = value.astype(BF16).reshape(nq, rows, tile)
            return carry

        lax.fori_loop(0, ff // tile, partial_sums, 0)

        def exchange(i, carry):
            to = lax.rem(q + i, nq)
            pltpu.make_async_remote_copy(
                src_ref=part.at[n, to],
                dst_ref=rsin.at[n, q],
                send_sem=r_send.at[n],
                recv_sem=r_recv.at[n],
                device_id=(to * 2 + c, e),
                device_id_type=MESH,
            ).start()
            return carry

        lax.fori_loop(1, nq, exchange, 0)
        copy = pltpu.make_async_remote_copy(
            src_ref=arr.at[n, 1 - c],
            dst_ref=sib.at[pl.ds(n * size, size)],
            send_sem=s_send.at[n],
            recv_sem=s_recv.at[n],
            device_id=(other, e),
            device_id_type=MESH,
        )
        copy.start()
        sibs.append(copy)
        rsin[n, q] = part[n, q]

    def gather_start(n):
        pltpu.make_async_copy(
            rsin.at[n, everyone], rsin.at[n, everyone], r_recv.at[n]
        ).wait()
        value = rsin[n, 0].astype(F32)
        for i in range(1, nq):
            value = value + rsin[n, i].astype(F32)
        hid[n, q] = value.astype(BF16)

        def share(i, carry):
            to = lax.rem(q + i, nq)
            pltpu.make_async_remote_copy(
                src_ref=hid.at[n, q],
                dst_ref=hid.at[n, q],
                send_sem=g_send.at[n],
                recv_sem=g_recv.at[n],
                device_id=(to * 2 + c, e),
                device_id_type=MESH,
            ).start()
            return carry

        lax.fori_loop(1, nq, share, 0)

    def return_start(n):
        if n == 0:
            weights[1].wait_recv()
            weights[2].wait_recv()
        pltpu.make_async_copy(
            hid.at[n, everyone], hid.at[n, everyone], g_recv.at[n]
        ).wait()
        dh = hid[n].astype(F32).reshape(size, ff)
        gate_grad = (dh * fac_g[pl.ds(n * size, size), :]).astype(BF16)
        up_grad = (dh * fac_u[pl.ds(n * size, size), :]).astype(BF16)
        for m in range(2):
            ret[n, m] = (nt(gate_grad, wg[m]) + nt(up_grad, wu[m])).astype(BF16)

        def give_back(i, carry):
            k = lax.rem(i, 2)
            turn = lax.div(i, 2)
            step = hop(n * turns + turn, lax.rem(z + c, 2))
            to = (yh + k - 2 * yh * k) * nz + lax.rem(z + step + nz, nz)
            target = back.at[pl.ds(pl.multiple_of(e * PAD, PAD), PAD)]
            for m in range(2):
                source = ret.at[n, m, pl.ds(pl.multiple_of(i * PAD, PAD), PAD)]
                remote = pltpu.make_async_remote_copy(
                    src_ref=source,
                    dst_ref=target,
                    send_sem=b_send,
                    recv_sem=b_recv,
                    device_id=(base + m, to),
                    device_id_type=MESH,
                )
                if n == chunks - 1:
                    mine = jnp.logical_and(to == e, c == m)

                    @pl.when(mine)
                    def _(source=source):
                        pltpu.make_async_copy(source, target, b_recv).start()

                    @pl.when(jnp.logical_not(mine))
                    def _(remote=remote):
                        remote.start()
                else:
                    remote.start()
            return carry

        lax.fori_loop(0, 2 * turns, give_back, 0)

    issue(2)
    reduce_start(0)
    gather_start(0)
    issue(3)
    return_start(0)
    reduce_start(1)
    gather_start(1)
    reduce_start(2)
    return_start(1)
    gather_start(2)
    reduce_start(3)
    return_start(2)
    gather_start(3)
    return_start(3)
    left(0)
    left(1)
    left(2)
    for copy in sibs:
        copy.wait_recv()
    own = jnp.concatenate([arr[n, c] for n in range(chunks)], axis=0)
    order = iota((1, total), 1)
    slot = iota((slots, total), 0)
    natural = (
        nn(onehot(slot_of(order, c) == slot), own)
        + nn(onehot(slot_of(order, 1 - c) == slot), sib[...])
    ).astype(BF16)

    def down(i, carry):
        f0 = pl.multiple_of(i * tile, tile)
        gdv[pl.ds(f0, tile), :] = nn(hact[pl.ds(f0, tile), :], natural).astype(BF16)
        return carry

    lax.fori_loop(0, ff // tile, down, 0)
    out = pltpu.make_async_copy(gdv, gd_hbm.at[0], l_sem.at[0])
    out.start()

    pltpu.make_async_copy(back, back, b_recv).wait()
    gx_ref[...] = nn(coll_t[...], back[...]).astype(BF16)

    out.wait()
    for copy in weights + sibs:
        copy.wait_send()
    for n in range(chunks):
        for sem in (r_send, g_send):
            pltpu.make_async_copy(
                rsin.at[n, everyone], rsin.at[n, everyone], sem.at[n]
            ).wait()
    ends = pl.ds(0, (4 * turns - 1) * PAD)
    less = pl.ds(0, (ne - 1) * PAD)

    @pl.when(h == c)
    def _():
        pltpu.make_async_copy(send.at[ends], send.at[ends], a_send.at[chunks - 1]).wait()
        pltpu.make_async_copy(send.at[less], send.at[less], b_send).wait()

    @pl.when(h != c)
    def _():
        left(chunks - 1)
        pltpu.make_async_copy(send, send, b_send).wait()


def finish(x_ref, d_ref, gx_ref, gd_ref, x_mem, d_mem, sem_in, sem_out):
    size = d_ref.shape[1] // PARTS
    blocks = [(x_ref, x_mem, gx_ref)]
    for i in range(PARTS):
        block = pl.ds(i * size, size)
        blocks.append((d_ref.at[:, block], d_mem.at[:, block], gd_ref.at[:, block]))
    fetches, writes = [], []
    for i, (src, mem, dst) in enumerate(blocks):
        fetches.append(pltpu.make_async_copy(src, mem, sem_in.at[i]))
        writes.append(pltpu.make_async_copy(mem, dst, sem_out.at[i]))
        fetches[i].start()
    for fetch, write in zip(fetches, writes):
        fetch.wait()
        write.start()
    for write in writes:
        write.wait()


def local(grad_out, routing, gates, scales, saved_gate, saved_up, w_gate, w_up, w_down):
    tok, dcols = grad_out.shape
    ne = lax.axis_size("expert")
    nq = lax.axis_size("dp") // 2
    nz = ne // 2
    _, ff, slots = saved_gate.shape
    cap = slots // ne
    chunks = min(4, nz // 2)
    size = nz * PAD // chunks
    rows = size // nq
    total = chunks * size
    vmem = pl.BlockSpec(memory_space=pltpu.VMEM)
    hbm = pl.BlockSpec(memory_space=pl.ANY)
    dma = pltpu.SemaphoreType.DMA
    tmp_x, tmp_d = pl.pallas_call(
        functools.partial(kernel, nz, cap),
        out_shape=(
            jax.ShapeDtypeStruct((tok, dcols), BF16),
            jax.ShapeDtypeStruct((1, ff, dcols), BF16),
        ),
        in_specs=[vmem] * 4 + [hbm] * 5,
        out_specs=(vmem, hbm),
        scratch_shapes=[
            pltpu.VMEM((ne * PAD, dcols), BF16),
            pltpu.VMEM((chunks, 2, size, dcols), BF16),
            pltpu.VMEM((total, dcols), BF16),
            pltpu.VMEM((ne * PAD, dcols), BF16),
            pltpu.VMEM((chunks, nq, rows, ff), BF16),
            pltpu.VMEM((chunks, nq, rows, ff), BF16),
            pltpu.VMEM((chunks, nq, rows, ff), BF16),
            pltpu.VMEM((total, ff), F32),
            pltpu.VMEM((total, ff), F32),
            pltpu.VMEM((ff, slots), BF16),
            pltpu.VMEM((ff, slots), BF16),
            pltpu.VMEM((ff, slots), BF16),
            pltpu.VMEM((2, dcols, ff), BF16),
            pltpu.VMEM((2, dcols, ff), BF16),
            pltpu.VMEM((2, ff, dcols), BF16),
            pltpu.VMEM((chunks, 2, size, dcols), BF16),
            pltpu.VMEM((ff, dcols), BF16),
            pltpu.VMEM((tok, ne * PAD), BF16),
            dma((chunks,)),
            dma((chunks,)),
            dma,
            dma,
            dma((chunks,)),
            dma((chunks,)),
            dma((chunks,)),
            dma((chunks,)),
            dma((3,)),
            dma((3,)),
            dma((chunks,)),
            dma((chunks,)),
            dma((5,)),
        ],
        compiler_params=pltpu.CompilerParams(
            collective_id=0, has_side_effects=True, vmem_limit_bytes=56 * 1024 * 1024
        ),
    )(
        grad_out,
        routing.T,
        gates.T,
        scales.reshape(1, tok),
        saved_gate,
        saved_up,
        w_gate,
        w_up,
        w_down,
    )
    return pl.pallas_call(
        finish,
        out_shape=(
            jax.ShapeDtypeStruct((tok, dcols), BF16),
            jax.ShapeDtypeStruct((1, ff, dcols), BF16),
        ),
        in_specs=[hbm, hbm],
        out_specs=(hbm, hbm),
        scratch_shapes=[
            pltpu.VMEM((tok, dcols), BF16),
            pltpu.VMEM((1, ff, dcols), BF16),
            dma((PARTS + 1,)),
            dma((PARTS + 1,)),
        ],
    )(tmp_x, tmp_d)


def solution(mesh):
    return jax.shard_map(
        local,
        mesh=mesh,
        in_specs=(
            P("expert", "dp"),
            P("expert", None),
            P("expert", None),
            P("expert"),
            P("expert", None, None),
            P("expert", None, None),
            P("expert", "dp", None),
            P("expert", "dp", None),
            P("expert", None, "dp"),
        ),
        out_specs=(P("expert", "dp"), P("expert", None, "dp")),
        check_vma=False,
    )
```

```python
import functools

import jax
import jax.numpy as jnp
from jax import lax
from jax.experimental import pallas as pl
from jax.experimental.pallas import tpu as pltpu
from jax.sharding import PartitionSpec as P

MESH = pl.DeviceIdType.MESH
PAD = 16
PARTS = 4
F32 = jnp.float32
BF16 = jnp.bfloat16


def nt(a, b):
    return lax.dot_general(a, b, (((1,), (1,)), ((), ())), preferred_element_type=F32)


def nn(a, b):
    return lax.dot_general(a, b, (((1,), (0,)), ((), ())), preferred_element_type=F32)


def iota(shape, dim):
    return lax.broadcasted_iota(jnp.int32, shape, dim)


def onehot(cond):
    return jnp.where(cond, 1.0, 0.0).astype(BF16)


def kernel(
    nz,
    cap,
    go_ref,
    rt_ref,
    gt_ref,
    sc_ref,
    sg_hbm,
    su_hbm,
    wg_hbm,
    wu_hbm,
    wd_hbm,
    gx_ref,
    gd_hbm,
    send,
    arr,
    sib,
    back,
    part,
    rsin,
    hid,
    fac_g,
    fac_u,
    sgv,
    suv,
    hact,
    wg,
    wu,
    wd,
    ret,
    gdv,
    coll_t,
    a_send,
    a_recv,
    b_send,
    b_recv,
    r_send,
    r_recv,
    g_send,
    g_recv,
    w_send,
    w_recv,
    s_send,
    s_recv,
    l_sem,
):
    tok, dcols = go_ref.shape
    topk = rt_ref.shape[0]
    ff, slots = sgv.shape
    ne = 2 * nz
    chunks, nq, rows, _ = part.shape
    size = nq * rows
    turns = size // (2 * PAD)
    dp = lax.axis_index("dp")
    e = lax.axis_index("expert")
    c = lax.rem(dp, 2)
    base = dp - c
    q = lax.div(dp, 2)
    yh = lax.div(e, nz)
    z = lax.rem(e, nz)
    h = lax.rem(z, 2)

    def hop(t, odd):
        far = nz // 2 - odd - 2 * ((t + 1 - odd) // 2)
        return far * (2 * ((t + odd) % 2) - 1)

    barrier = pltpu.get_barrier_semaphore()

    def greet(i, carry):
        step = lax.div(i + 1, 2) * (2 * lax.rem(i, 2) - 1)
        zt = lax.rem(z + nz // 2 + step + nz, nz)
        for yt in range(2):
            there = yt * nz + zt

            @pl.when(jnp.logical_or(there != e, h != c))
            def _(there=there):
                pl.semaphore_signal(
                    barrier, inc=1, device_id=(base + h, there), device_id_type=MESH
                )

            @pl.when(
                jnp.logical_and(
                    lax.rem(zt, 2) == c, jnp.logical_or(there != e, h == c)
                )
            )
            def _(there=there):
                pl.semaphore_signal(
                    barrier, inc=1, device_id=(base + 1 - h, there), device_id_type=MESH
                )

        return carry

    lax.fori_loop(0, nz, greet, 0)
    for i in range(1, nq):
        pl.semaphore_signal(
            barrier,
            inc=1,
            device_id=(lax.rem(q + i, nq) * 2 + c, e),
            device_id_type=MESH,
        )

    loads = [
        pltpu.make_async_copy(sg_hbm.at[0], sgv, l_sem.at[0]),
        pltpu.make_async_copy(su_hbm.at[0], suv, l_sem.at[1]),
        pltpu.make_async_copy(wd_hbm.at[0], wd.at[c], l_sem.at[2]),
        pltpu.make_async_copy(wg_hbm.at[0], wg.at[c], l_sem.at[3]),
        pltpu.make_async_copy(wu_hbm.at[0], wu.at[c], l_sem.at[4]),
    ]
    for copy in loads:
        copy.start()

    row_e = iota((ne, tok), 0)
    named = jnp.zeros((ne, tok), F32)
    gate = jnp.zeros((ne, tok), F32)
    for k in range(topk):
        hit = rt_ref[k : k + 1, :] == row_e
        named = named + jnp.where(hit, 1.0, 0.0)
        gate = gate + jnp.where(hit, gt_ref[k : k + 1, :], 0.0)
    earlier = onehot(iota((tok, tok), 0) < iota((tok, tok), 1))
    value = named * (nn(named.astype(BF16), earlier) + 1.0)
    spread = (iota((ne * PAD, ne), 0) // PAD) == iota((ne * PAD, ne), 1)
    wanted = ((iota((ne * PAD, tok), 0) % PAD) + 1).astype(F32)
    pick = nn(onehot(spread), value.astype(BF16)) == wanted
    gates_at = lax.dot_general(
        jnp.where(spread, 1.0, 0.0),
        gate,
        (((1,), (0,)), ((), ())),
        precision=lax.Precision.HIGHEST,
        preferred_element_type=F32,
    )
    slot_factor = jnp.sum(
        jnp.where(pick, gates_at * sc_ref[...], 0.0), axis=1, keepdims=True
    )
    owned = nn(onehot(pick), go_ref[...])
    send[...] = (slot_factor * owned).astype(BF16)

    pl.semaphore_wait(barrier, ne + ne // 2 + nq - 1 - jnp.where(h == c, 1, 0))

    other = base + 1 - c

    def scatter(i, carry, n, last):
        k = lax.rem(i, 2)
        odd = lax.rem(lax.div(i, 2), 2)
        turn = lax.div(i, 4)
        step = hop(n * turns + turn, odd)
        to = (yh + k - 2 * yh * k) * nz + lax.rem(z - step + nz, nz)
        source = send.at[pl.ds(pl.multiple_of(to * PAD, PAD), PAD)]
        place = pl.multiple_of((turn * 2 + k) * PAD, PAD)
        target = arr.at[n, c, pl.ds(place, PAD)]
        remote = pltpu.make_async_remote_copy(
            src_ref=source,
            dst_ref=target,
            send_sem=a_send.at[n],
            recv_sem=a_recv.at[n],
            device_id=(base + h, to),
            device_id_type=MESH,
        )
        if last:
            mine = jnp.logical_and(to == e, h == c)

            @pl.when(mine)
            def _():
                pltpu.make_async_copy(source, target, a_recv.at[n]).start()

            @pl.when(jnp.logical_not(mine))
            def _():
                remote.start()
        else:
            remote.start()
        return carry

    def issue(n):
        last = n == chunks - 1
        lax.fori_loop(0, 4 * turns, functools.partial(scatter, n=n, last=last), 0)

    def left(n):
        out = pl.ds(0, 4 * turns * PAD)
        pltpu.make_async_copy(send.at[out], send.at[out], a_send.at[n]).wait()

    issue(0)
    weights = []
    for n, (src, dst) in enumerate(((wd_hbm, wd), (wg_hbm, wg), (wu_hbm, wu))):
        copy = pltpu.make_async_remote_copy(
            src_ref=src.at[0],
            dst_ref=dst.at[c],
            send_sem=w_send.at[n],
            recv_sem=w_recv.at[n],
            device_id=(other, e),
            device_id_type=MESH,
        )
        copy.start()
        weights.append(copy)

    spread_t = iota((ne, ne * PAD), 0) == (iota((ne, ne * PAD), 1) // PAD)
    wanted_t = ((iota((tok, ne * PAD), 1) % PAD) + 1).astype(F32)
    coll_t[...] = onehot(nn(value.T.astype(BF16), onehot(spread_t)) == wanted_t)

    loads[0].wait()
    loads[1].wait()

    def slot_of(index, core):
        k = (index // PAD) % 2
        odd = lax.rem(z + core, 2)
        zt = (z + hop(index // (2 * PAD), odd) + nz) % nz
        g = (yh + k - 2 * yh * k) * nz + zt
        place = index % PAD
        return jnp.where(place < cap, g * cap + place, -1)

    total = chunks * size
    take = onehot(slot_of(iota((total, 1), 0), c) == iota((total, slots), 1))
    tile = 128

    def factors(i, carry):
        f0 = pl.multiple_of(i * tile, tile)
        g = nt(take, sgv[pl.ds(f0, tile), :])
        u = nt(take, suv[pl.ds(f0, tile), :])
        sig = jax.nn.sigmoid(g)
        fac_g[:, pl.ds(f0, tile)] = u * sig * (1.0 + g * (1.0 - sig))
        fac_u[:, pl.ds(f0, tile)] = g * sig
        return carry

    lax.fori_loop(0, ff // tile, factors, 0)
    issue(1)

    def activate(i, carry):
        f0 = pl.multiple_of(i * 32, 32)
        g = sgv[pl.ds(f0, 32), :].astype(F32)
        u = suv[pl.ds(f0, 32), :].astype(F32)
        hact[pl.ds(f0, 32), :] = (g * jax.nn.sigmoid(g) * u).astype(BF16)
        return carry

    lax.fori_loop(0, ff // 32, activate, 0)

    for copy in loads[2:]:
        copy.wait()

    sibs = []
    everyone = pl.ds(0, nq - 1)
    partners = sorted(range(1, nq), key=lambda i: i % 4 != 2)

    def reduce_start(n):
        pltpu.make_async_copy(arr.at[n], arr.at[n], a_recv.at[n]).wait()
        if n == 0:
            weights[0].wait_recv()

        def partial_sums(i, carry):
            f0 = pl.multiple_of(i * tile, tile)
            value = nt(arr[n, 0], wd[0, pl.ds(f0, tile), :]) + nt(
                arr[n, 1], wd[1, pl.ds(f0, tile), :]
            )
            part[n, :, :, pl.ds(f0, tile)] = value.astype(BF16).reshape(nq, rows, tile)
            return carry

        lax.fori_loop(0, ff // tile, partial_sums, 0)

        for i in partners:
            to = lax.rem(q + i, nq)
            pltpu.make_async_remote_copy(
                src_ref=part.at[n, to],
                dst_ref=rsin.at[n, q],
                send_sem=r_send.at[n],
                recv_sem=r_recv.at[n],
                device_id=(to * 2 + c, e),
                device_id_type=MESH,
            ).start()
        copy = pltpu.make_async_remote_copy(
            src_ref=arr.at[n, 1 - c],
            dst_ref=sib.at[pl.ds(n * size, size)],
            send_sem=s_send.at[n],
            recv_sem=s_recv.at[n],
            device_id=(other, e),
            device_id_type=MESH,
        )
        copy.start()
        sibs.append(copy)
        rsin[n, q] = part[n, q]

    def gather_start(n):
        pltpu.make_async_copy(
            rsin.at[n, everyone], rsin.at[n, everyone], r_recv.at[n]
        ).wait()
        value = rsin[n, 0].astype(F32)
        for i in range(1, nq):
            value = value + rsin[n, i].astype(F32)
        hid[n, q] = value.astype(BF16)

        for i in partners:
            to = lax.rem(q + i, nq)
            pltpu.make_async_remote_copy(
                src_ref=hid.at[n, q],
                dst_ref=hid.at[n, q],
                send_sem=g_send.at[n],
                recv_sem=g_recv.at[n],
                device_id=(to * 2 + c, e),
                device_id_type=MESH,
            ).start()

    def return_start(n):
        if n == 0:
            weights[1].wait_recv()
            weights[2].wait_recv()
        pltpu.make_async_copy(
            hid.at[n, everyone], hid.at[n, everyone], g_recv.at[n]
        ).wait()
        dh = hid[n].astype(F32).reshape(size, ff)
        gate_grad = (dh * fac_g[pl.ds(n * size, size), :]).astype(BF16)
        up_grad = (dh * fac_u[pl.ds(n * size, size), :]).astype(BF16)
        for m in range(2):
            ret[n, m] = (nt(gate_grad, wg[m]) + nt(up_grad, wu[m])).astype(BF16)

        def give_back(i, carry):
            k = lax.rem(i, 2)
            turn = lax.div(i, 2)
            step = hop(n * turns + turn, lax.rem(z + c, 2))
            to = (yh + k - 2 * yh * k) * nz + lax.rem(z + step + nz, nz)
            target = back.at[pl.ds(pl.multiple_of(e * PAD, PAD), PAD)]
            for m in range(2):
                source = ret.at[n, m, pl.ds(pl.multiple_of(i * PAD, PAD), PAD)]
                remote = pltpu.make_async_remote_copy(
                    src_ref=source,
                    dst_ref=target,
                    send_sem=b_send,
                    recv_sem=b_recv,
                    device_id=(base + m, to),
                    device_id_type=MESH,
                )
                if n == chunks - 1:
                    mine = jnp.logical_and(to == e, c == m)

                    @pl.when(mine)
                    def _(source=source):
                        pltpu.make_async_copy(source, target, b_recv).start()

                    @pl.when(jnp.logical_not(mine))
                    def _(remote=remote):
                        remote.start()
                else:
                    remote.start()
            return carry

        lax.fori_loop(0, 2 * turns, give_back, 0)

    issue(2)
    issue(3)
    reduce_start(0)
    gather_start(0)
    return_start(0)
    reduce_start(1)
    gather_start(1)
    reduce_start(2)
    return_start(1)
    gather_start(2)
    reduce_start(3)
    return_start(2)
    gather_start(3)
    return_start(3)
    left(0)
    left(1)
    left(2)
    for copy in sibs:
        copy.wait_recv()
    own = jnp.concatenate([arr[n, c] for n in range(chunks)], axis=0)
    order = iota((1, total), 1)
    slot = iota((slots, total), 0)
    natural = (
        nn(onehot(slot_of(order, c) == slot), own)
        + nn(onehot(slot_of(order, 1 - c) == slot), sib[...])
    ).astype(BF16)

    def down(i, carry):
        f0 = pl.multiple_of(i * tile, tile)
        gdv[pl.ds(f0, tile), :] = nn(hact[pl.ds(f0, tile), :], natural).astype(BF16)
        return carry

    lax.fori_loop(0, ff // tile, down, 0)
    out = pltpu.make_async_copy(gdv, gd_hbm.at[0], l_sem.at[0])
    out.start()

    pltpu.make_async_copy(back, back, b_recv).wait()
    gx_ref[...] = nn(coll_t[...], back[...]).astype(BF16)

    out.wait()
    for copy in weights + sibs:
        copy.wait_send()
    for n in range(chunks):
        for sem in (r_send, g_send):
            pltpu.make_async_copy(
                rsin.at[n, everyone], rsin.at[n, everyone], sem.at[n]
            ).wait()
    ends = pl.ds(0, (4 * turns - 1) * PAD)
    less = pl.ds(0, (ne - 1) * PAD)

    @pl.when(h == c)
    def _():
        pltpu.make_async_copy(send.at[ends], send.at[ends], a_send.at[chunks - 1]).wait()
        pltpu.make_async_copy(send.at[less], send.at[less], b_send).wait()

    @pl.when(h != c)
    def _():
        left(chunks - 1)
        pltpu.make_async_copy(send, send, b_send).wait()


def finish(x_ref, d_ref, gx_ref, gd_ref, x_mem, d_mem, sem_in, sem_out):
    size = d_ref.shape[1] // PARTS
    blocks = [(x_ref, x_mem, gx_ref)]
    for i in range(PARTS):
        block = pl.ds(i * size, size)
        blocks.append((d_ref.at[:, block], d_mem.at[:, block], gd_ref.at[:, block]))
    fetches, writes = [], []
    for i, (src, mem, dst) in enumerate(blocks):
        fetches.append(pltpu.make_async_copy(src, mem, sem_in.at[i]))
        writes.append(pltpu.make_async_copy(mem, dst, sem_out.at[i]))
        fetches[i].start()
    for fetch, write in zip(fetches, writes):
        fetch.wait()
        write.start()
    for write in writes:
        write.wait()


def local(grad_out, routing, gates, scales, saved_gate, saved_up, w_gate, w_up, w_down):
    tok, dcols = grad_out.shape
    ne = lax.axis_size("expert")
    nq = lax.axis_size("dp") // 2
    nz = ne // 2
    _, ff, slots = saved_gate.shape
    cap = slots // ne
    chunks = min(4, nz // 2)
    size = nz * PAD // chunks
    rows = size // nq
    total = chunks * size
    vmem = pl.BlockSpec(memory_space=pltpu.VMEM)
    hbm = pl.BlockSpec(memory_space=pl.ANY)
    dma = pltpu.SemaphoreType.DMA
    tmp_x, tmp_d = pl.pallas_call(
        functools.partial(kernel, nz, cap),
        out_shape=(
            jax.ShapeDtypeStruct((tok, dcols), BF16),
            jax.ShapeDtypeStruct((1, ff, dcols), BF16),
        ),
        in_specs=[vmem] * 4 + [hbm] * 5,
        out_specs=(vmem, hbm),
        scratch_shapes=[
            pltpu.VMEM((ne * PAD, dcols), BF16),
            pltpu.VMEM((chunks, 2, size, dcols), BF16),
            pltpu.VMEM((total, dcols), BF16),
            pltpu.VMEM((ne * PAD, dcols), BF16),
            pltpu.VMEM((chunks, nq, rows, ff), BF16),
            pltpu.VMEM((chunks, nq, rows, ff), BF16),
            pltpu.VMEM((chunks, nq, rows, ff), BF16),
            pltpu.VMEM((total, ff), F32),
            pltpu.VMEM((total, ff), F32),
            pltpu.VMEM((ff, slots), BF16),
            pltpu.VMEM((ff, slots), BF16),
            pltpu.VMEM((ff, slots), BF16),
            pltpu.VMEM((2, dcols, ff), BF16),
            pltpu.VMEM((2, dcols, ff), BF16),
            pltpu.VMEM((2, ff, dcols), BF16),
            pltpu.VMEM((chunks, 2, size, dcols), BF16),
            pltpu.VMEM((ff, dcols), BF16),
            pltpu.VMEM((tok, ne * PAD), BF16),
            dma((chunks,)),
            dma((chunks,)),
            dma,
            dma,
            dma((chunks,)),
            dma((chunks,)),
            dma((chunks,)),
            dma((chunks,)),
            dma((3,)),
            dma((3,)),
            dma((chunks,)),
            dma((chunks,)),
            dma((5,)),
        ],
        compiler_params=pltpu.CompilerParams(
            collective_id=0, has_side_effects=True, vmem_limit_bytes=56 * 1024 * 1024
        ),
    )(
        grad_out,
        routing.T,
        gates.T,
        scales.reshape(1, tok),
        saved_gate,
        saved_up,
        w_gate,
        w_up,
        w_down,
    )
    return pl.pallas_call(
        finish,
        out_shape=(
            jax.ShapeDtypeStruct((tok, dcols), BF16),
            jax.ShapeDtypeStruct((1, ff, dcols), BF16),
        ),
        in_specs=[hbm, hbm],
        out_specs=(hbm, hbm),
        scratch_shapes=[
            pltpu.VMEM((tok, dcols), BF16),
            pltpu.VMEM((1, ff, dcols), BF16),
            dma((PARTS + 1,)),
            dma((PARTS + 1,)),
        ],
    )(tmp_x, tmp_d)


def solution(mesh):
    return jax.shard_map(
        local,
        mesh=mesh,
        in_specs=(
            P("expert", "dp"),
            P("expert", None),
            P("expert", None),
            P("expert"),
            P("expert", None, None),
            P("expert", None, None),
            P("expert", "dp", None),
            P("expert", "dp", None),
            P("expert", None, "dp"),
        ),
        out_specs=(P("expert", "dp"), P("expert", None, "dp")),
        check_vma=False,
    )
```
